32 devices in a mesh: group: 4 (over y, x), dev: 8 (over z, core).
Axes of the slice: x: 2, y: 2, z: 4, core: 2. Of those that a mesh axis runs over, the one named last changes fastest.
Arguments:
- density: float32 [32, 320, 128], P(('group', 'dev')), may hold values from 0.5 to 2
- velocity: float32 [3, 32, 320, 128], P(None, ('group', 'dev')), may hold values from -0.75 to 0.75
- pressure: float32 [32, 320, 128], P(('group', 'dev')), may hold values from 0.5 to 2
- rbf_blocks: bfloat16 [2048, 128, 128], P(('group', 'dev')), may hold values from -0.5 to 0.5
- correlation: int32 [2048, 128], P(('group', 'dev')), may hold values from 0 to 319
- normals: float32 [2048, 3, 128], P(('group', 'dev')), may hold values from -6 to 6
- routes: int32 [2048, 1], P(('group', 'dev')), may hold values from 0 to 31; in each aligned block of 64 rows (0 to 63, 64 to 127, ...) at most 4 rows name the same one
- targets: int32 [2048], P(('group', 'dev')), may hold values from 0 to 31
- stiffness: bfloat16 [1024, 128, 128], P(('group', 'dev')), may hold values from -0.35 to 2.35
- coupling: bfloat16 [1024, 128, 128], P(('group', 'dev')), may hold values from -0.5 to 0.5
- inverse_diag: float32 [1024, 3, 128], P(('group', 'dev')), may hold values from 0.5 to 1.5
- displacement: float32 [1024, 3, 128], P(('group', 'dev')), may hold values from -6 to 6
- diff_res: float32 [8, 1024, 3, 128], P(None, ('group', 'dev')), may hold values from -2 to 2
- diff_disp: float32 [8, 1024, 3, 128], P(None, ('group', 'dev')), may hold values from -2.4 to 2.4
Outputs:
- fluid_next: float32 [5, 32, 320, 128], P(None, ('group', 'dev'))
- disp_next: float32 [1024, 3, 128], P(('group', 'dev'))
- wall_motion: float32 [2048, 3, 128], P(('group', 'dev'))
The draws below stay inside these ranges and needn't reach their ends.
Inputs may be any that keep to these rules, and one draw needn't show every extreme that they name: `routes`: among the 64 blocks of one device at most 4 name the same owner, and some device names one owner exactly 4 times.
All inputs are finite; a program needn't handle non-finite values.
Results may differ from the reference program's by a relative error of at most 0.0004.
The reference program's roundings to bfloat16 on the way (of `weighted` and `disp_half`) count: a program that leaves them out, or rounds other values in their place, can miss the bound.
Values may be sent and summed in bfloat16 or wider, within the bound.
A program may use at most 64 MiB of HBM per device.

```python
import math
import jax
import jax.numpy as jnp
import numpy as np
from jax import lax

CX = 1
CY = 320
CZ = 128
NB = 64
NS = 32
NODES = 128
M = 8
CAP = 4
NX = 32
NBT = 2048
NST = 1024
DEVICES = 32


def newton_parts(key):
    subkeys = jax.random.split(jax.random.fold_in(key, 4099), 7)
    position = (jnp.arange(NST, dtype=jnp.float32) / NST)[None, :, None, None]
    extent = (M, NST, 3, NODES)
    spread = 0.15 * jnp.power(3.0, position)
    private = jnp.clip(jax.random.normal(subkeys[0], extent, jnp.float32), -4.0, 4.0)
    shared = jnp.clip(jax.random.normal(subkeys[1], (1, NST, 3, NODES), jnp.float32), -4.0, 4.0)
    columns = spread * (private + 0.5 * shared)
    resting = 0.5 * jnp.clip(jax.random.normal(subkeys[2], (NST, 3, NODES), jnp.float32), -4.0, 4.0)
    columns = jnp.clip(columns, -2.0, 2.0)
    lead_signs = jnp.where(jax.random.bernoulli(subkeys[3], 0.5, (M,)), 1.0, -1.0)
    growth_signs = jnp.where(jax.random.bernoulli(subkeys[4], 0.5, (M,)), 1.0, -1.0)
    leading = lead_signs * jax.random.uniform(subkeys[5], (M,), jnp.float32, 0.3, 0.8)
    growth = growth_signs * jax.random.uniform(subkeys[6], (M,), jnp.float32, 0.4, 0.8)
    weights = leading[:, None, None, None] + growth[:, None, None, None] * position
    settled = jnp.clip(resting + jnp.sum(weights * columns, axis=0), -6.0, 6.0)
    return (columns, settled)


def draw_diff_res(key, part):
    return newton_parts(key)[0]


def draw_displacement(key, part):
    return newton_parts(key)[1]


def draw_stiffness(key, part):
    noise_key = jax.random.fold_in(key, 8191)
    offdiag = jnp.clip(jax.random.normal(noise_key, (NST, NODES, NODES), jnp.float32) / math.sqrt(NODES), -0.35, 0.35)
    return (2.0 * jnp.eye(NODES, dtype=jnp.float32)[None] + offdiag).astype(jnp.bfloat16)


def plant(result, own_key, low, top_value):
    index_at = [jax.random.randint(jax.random.fold_in(own_key, axis), (), 0, length) for axis, length in enumerate(result.shape)]
    longest = result.shape.index(max(result.shape))
    neighbour = index_at[:longest] + [(index_at[longest] + 1) % result.shape[longest]] + index_at[longest + 1:]
    return result.at[tuple(index_at)].set(low).at[tuple(neighbour)].set(top_value)


def block_scale(key, dims, cuts, least, top_value):
    level = 1.0
    for dim, blocks in cuts:
        heights = jax.random.uniform(jax.random.fold_in(jax.random.fold_in(key, 6), dim), (blocks,), jnp.float32, least / len(cuts), top_value / len(cuts))
        level = level * jnp.repeat(jnp.exp(heights), dims[dim] // blocks).reshape((-1,) + (1,) * (len(dims) - 1 - dim))
    return level


def routed_block(stream_key, own, number, rows, amount, top, bound, lean):
    ranking = jax.random.permutation(stream_key, amount)
    packed, ordinary = shares(amount, rows * top, bound, lean, True), shares(amount, rows * top, bound, lean, False)
    places = jnp.arange(amount)

    def named(sizes, offset_by):
        used = int((sizes > 0).sum())
        fixed = max(1, used // 4)
        passed = fixed + (places - fixed + offset_by * (used - fixed)) % max(1, amount - fixed)
        return jnp.zeros((amount,), jnp.int32).at[ranking[jnp.where(places < fixed, places, passed)]].set(jnp.asarray(sizes, jnp.int32))

    sizes = jnp.where(number % 4 == 0, named(packed, number // 4), named(ordinary, number - number // 4 - 1))
    mixed = jax.random.permutation(jax.random.fold_in(own, 3), amount)
    donor, sink = mixed[0:amount // 2 * 2:2], mixed[1:amount // 2 * 2:2]
    room = jnp.minimum(sizes[donor] - 1, bound - sizes[sink]) // 2
    room = jnp.where((donor == ranking[0]) | (sink == ranking[0]) | (sizes[sink] == 0), 0, jnp.maximum(room, 0))
    passed = jax.random.randint(jax.random.fold_in(own, 4), (amount // 2,), 0, 1 << 20) % (room + 1)
    sizes = sizes.at[donor].add(-passed).at[sink].add(passed)
    labels = jnp.searchsorted(jnp.cumsum(sizes), jnp.arange(rows * top), side="right").astype(jnp.int32)
    grid = labels.reshape(top, rows).T
    grid = grid[jax.random.permutation(jax.random.fold_in(own, 1), rows)]
    offset_by = jax.random.randint(jax.random.fold_in(own, 2), (rows, 1), 0, top)
    return jnp.take_along_axis(grid, (jnp.arange(top)[None, :] + offset_by) % top, axis=1)


def shares(count, total, most, skew, full):
    loads = [(1 << 20) // math.isqrt(rank ** skew) + 1 for rank in range(1, count + 1)]
    largest = most if full else min(most, max(-(-total // count), total * loads[0] // sum(loads)))
    least = 1 if total - largest >= count - 1 else 0
    counts, spare = [largest] + [least] * (count - 1), total - largest - least * (count - 1)
    while spare > 0:
        movable = [i for i in range(1, count) if counts[i] < largest] or [i for i in range(1, count) if counts[i] < most]
        whole, left = sum([loads[i] for i in movable]), spare
        for i in movable:
            addition = min(most - counts[i], max(1, left * loads[i] // whole), spare)
            counts[i] = counts[i] + addition
            spare = spare - addition
    return np.array(counts)


def gaussian(key, shape, width, most, pieces=(), kind=jnp.bfloat16):
    entries = width * jax.random.normal(key, shape, jnp.float32)
    if pieces:
        entries = entries * block_scale(key, shape, pieces, -0.22, 0.18)
    return jnp.clip(entries, -most, most).astype(kind)


def setup_inputs(seed: int = 0) -> dict:
    key_list = jax.random.split(jax.random.key(seed), 15)
    density = jnp.clip(jnp.exp(math.log(2.0) - 1.3862944 * jax.random.uniform(key_list[0], (NX, CY, CZ), jnp.float32) ** block_scale(key_list[0], (NX, CY, CZ), ((0, 32),), -0.2, 0.2)), 0.5, 2.0)
    velocity = gaussian(key_list[1], (3, NX, CY, CZ), 0.3, 0.75, ((1, 32),), jnp.float32)
    pressure = jnp.clip(jnp.exp(math.log(2.0) - 1.3862944 * jax.random.uniform(key_list[2], (NX, CY, CZ), jnp.float32) ** block_scale(key_list[2], (NX, CY, CZ), ((0, 32),), -0.2, 0.2)), 0.5, 2.0)
    rbf_blocks = gaussian(key_list[3], (NBT, NODES, NODES), NODES ** -0.5, 0.5, ((0, 32),))
    correlation = plant(jax.random.randint(key_list[4], (NBT, NODES), 0, CX * CY), jax.random.fold_in(key_list[4], 1), 0, (CX * CY) - 1).astype(jnp.int32)
    normals = gaussian(key_list[5], (NBT, 3, NODES), 1.0, 6.0, ((0, 32),), jnp.float32)
    routes_keys = jax.random.split(jax.random.fold_in(key_list[6], 1), NBT // NB)
    routes_turns = jax.random.permutation(jax.random.fold_in(key_list[6], 3), NBT // NB)
    routes = jax.vmap(lambda own, number: routed_block(jax.random.fold_in(key_list[6], 2), own, number, NB, DEVICES, 1, CAP, 2))(routes_keys, routes_turns).reshape((NBT, 1))
    targets = plant(jax.random.randint(key_list[7], (NBT,), 0, NS), jax.random.fold_in(key_list[7], 1), 0, NS - 1).astype(jnp.int32)
    stiffness = draw_stiffness(jax.random.fold_in(key_list[14], 71), 0)
    coupling = gaussian(key_list[9], (NST, NODES, NODES), NODES ** -0.5, 0.5, ((0, 32),))
    inverse_diag = jnp.clip(1.0 + 0.1 * jax.random.normal(key_list[10], (NST, 3, NODES), jnp.float32), 0.5, 1.5)
    displacement = draw_displacement(jax.random.fold_in(key_list[14], 71), 0)
    diff_res = draw_diff_res(jax.random.fold_in(key_list[14], 71), 0)
    diff_disp = gaussian(key_list[13], (M, NST, 3, NODES), 0.4, 2.4, ((1, 32),), jnp.float32)
    return {"density": density, "velocity": velocity, "pressure": pressure, "rbf_blocks": rbf_blocks, "correlation": correlation, "normals": normals, "routes": routes, "targets": targets, "stiffness": stiffness, "coupling": coupling, "inverse_diag": inverse_diag, "displacement": displacement, "diff_res": diff_res, "diff_disp": diff_disp}


ratio_heat = 1.4
step_ratio = 0.03

def euler_flux(state, normal_axis):
    dens = state[0]
    vel = state[1:4] / dens
    press = (ratio_heat - 1.0) * (state[4] - 0.5 * dens * lax.optimization_barrier(jnp.sum(vel * vel, axis=0)))
    normal_speed = vel[normal_axis]
    rows = [dens * normal_speed]
    for comp in range(3):
        moment = state[1 + comp] * normal_speed
        if comp == normal_axis:
            moment = moment + press
        rows.append(moment)
    rows.append((state[4] + press) * normal_speed)
    wave_speed = jnp.abs(normal_speed) + jnp.sqrt(ratio_heat * press / dens)
    return (jnp.stack(rows, axis=0), wave_speed)

def rusanov(left_state, right_state, normal_axis):
    flux_left, speed_left = euler_flux(left_state, normal_axis)
    flux_right, speed_right = euler_flux(right_state, normal_axis)
    return 0.5 * (flux_left + flux_right) - 0.5 * jnp.maximum(speed_left, speed_right) * (right_state - left_state)

def conserve(density, velocity, pressure):
    energy = pressure / (ratio_heat - 1.0) + 0.5 * density * lax.optimization_barrier(jnp.sum(velocity * velocity, axis=0))
    return jnp.concatenate([density[None], density[None] * velocity, energy[None]], axis=0)

def advance(padded, conserved):
    face_x = rusanov(padded[:, :-1], padded[:, 1:], 0)
    divergence = face_x[:, 1:] - face_x[:, :-1]
    face_y = rusanov(conserved, jnp.roll(conserved, -1, axis=2), 1)
    divergence = divergence + face_y - jnp.roll(face_y, 1, axis=2)
    mirror_sign = jnp.array([1.0, 1.0, 1.0, -1.0, 1.0], dtype=conserved.dtype)[:, None, None, None]
    padded_z = jnp.concatenate([conserved[..., :1] * mirror_sign, conserved, conserved[..., -1:]], axis=3)
    face_z = rusanov(padded_z[..., :-1], padded_z[..., 1:], 2)
    divergence = divergence + face_z[..., 1:] - face_z[..., :-1]
    return conserved - step_ratio * divergence

def wall_pressure(state):
    bottom = state[..., 0]
    return (ratio_heat - 1.0) * (bottom[4] - 0.5 * lax.optimization_barrier(jnp.sum(bottom[1:4] * bottom[1:4], axis=0)) / bottom[0])

def cho_apply(gram, projected):
    factor = jnp.linalg.cholesky(gram)
    middle = lax.linalg.triangular_solve(factor, projected[:, None], left_side=True, lower=True)
    return lax.linalg.triangular_solve(factor, middle, left_side=True, lower=True, transpose_a=True)[:, 0]

def reference(density, velocity, pressure, rbf_blocks, correlation, normals, routes, targets, stiffness, coupling, inverse_diag, displacement, diff_res, diff_disp):
    row_offsets = jnp.arange(CX + 2, dtype=jnp.int32)

    def slab_step(index, carry):
        fluid_all, wall_all = carry
        slab_index = jnp.asarray(index).astype(jnp.int32)
        start = (slab_index * CX).astype(jnp.int32)
        row_ids = ((start - 1 + row_offsets) % NX).astype(jnp.int32)
        piece = conserve(jnp.take(density, row_ids, axis=0), jnp.take(velocity, row_ids, axis=1), jnp.take(pressure, row_ids, axis=0))
        slab = advance(piece, piece[:, 1:-1])
        fluid_all = lax.dynamic_update_slice_in_dim(fluid_all, slab, start, 1)
        wall_all = lax.dynamic_update_slice_in_dim(wall_all, wall_pressure(slab).reshape(1, CX * CY), slab_index, 0)
        return (fluid_all, wall_all)
    fluid_start = jnp.zeros((5, NX, CY, CZ), jnp.float32)
    wall_start = jnp.zeros((DEVICES, CX * CY), jnp.float32)
    fluid_next, wall_rows = lax.fori_loop(0, DEVICES, slab_step, (fluid_start, wall_start))

    def map_loads(element):
        wall_row, indices, normal_rows, kernels = element
        weighted = (wall_row[indices][:, None, :] * normal_rows).astype(jnp.bfloat16)
        return jnp.einsum('bci,bij->bcj', weighted.astype(jnp.float32), kernels.astype(jnp.float32))
    block_load = lax.map(map_loads, (wall_rows, correlation.reshape(DEVICES, NB, NODES), normals.reshape(DEVICES, NB, 3, NODES), rbf_blocks.reshape(DEVICES, NB, NODES, NODES)))
    block_load = block_load.reshape(NBT, 3, NODES)
    solid_ids = (routes[:, 0] * NS + targets).astype(jnp.int32)
    solid_load = jax.ops.segment_sum(block_load, solid_ids, num_segments=NST)
    disp_half = displacement.astype(jnp.bfloat16)
    earlier = jnp.concatenate([jnp.zeros((1, 3, NODES), jnp.bfloat16), disp_half[:-1]], axis=0)
    solid_res = jnp.einsum('bcj,bij->bci', disp_half.astype(jnp.float32), stiffness.astype(jnp.float32))
    solid_res = solid_res + jnp.einsum('bcj,bij->bci', earlier.astype(jnp.float32), coupling.astype(jnp.float32)) - solid_load
    coupling_res = -inverse_diag * solid_res
    gram = jnp.einsum('mbcj,nbcj->mn', diff_res, diff_res, precision=lax.Precision.HIGHEST)
    projected = jnp.einsum('mbcj,bcj->m', diff_res, coupling_res, precision=lax.Precision.HIGHEST)
    mixing = -cho_apply(gram, projected)
    disp_next = displacement + coupling_res + jnp.einsum('mbcj,m->bcj', diff_disp, mixing, precision=lax.Precision.HIGHEST)
    reply = disp_next.astype(jnp.bfloat16)[solid_ids]

    def map_motion(element):
        kernels, rows = element
        return jnp.einsum('bij,bcj->bci', kernels.astype(jnp.float32), rows.astype(jnp.float32))
    wall_motion = lax.map(map_motion, (rbf_blocks.reshape(DEVICES, NB, NODES, NODES), reply.reshape(DEVICES, NB, 3, NODES)))
    return (fluid_next, disp_next, wall_motion.reshape(NBT, 3, NODES))
```

```python
import jax
import jax.numpy as jnp
from jax import lax
from jax.experimental import pallas as pl
from jax.experimental.pallas import tpu as pltpu
from jax.sharding import PartitionSpec as P

ratio_heat = 1.4
step_ratio = 0.03


def extended(value, sides, width):
    for axis, dim in sides:
        peers, length = (lax.axis_size(axis), value.shape[dim])
        up = [(i, (i + 1) % peers) for i in range(peers)]
        down = [(j, i) for i, j in up]
        last = lax.slice_in_dim(value, length - width, length, axis=dim)
        leading = lax.slice_in_dim(value, 0, width, axis=dim)
        before = lax.ppermute(last, axis, up)
        after = lax.ppermute(leading, axis, down)
        value = jnp.concatenate([before, value, after], axis=dim)
    return value


def shifted(block, axis, distance):
    devices = range(lax.axis_size(axis))
    route = [(i - distance, i) for i in devices if i - distance in devices]
    return lax.ppermute(block, axis, route)


def euler_flux(state, normal_axis):
    dens = state[0]
    vel = state[1:4] / dens
    press = (ratio_heat - 1.0) * (state[4] - 0.5 * dens * jnp.sum(vel * vel, axis=0))
    normal_speed = vel[normal_axis]
    rows = [dens * normal_speed]
    for comp in range(3):
        moment = state[1 + comp] * normal_speed
        if comp == normal_axis:
            moment = moment + press
        rows.append(moment)
    rows.append((state[4] + press) * normal_speed)
    wave_speed = jnp.abs(normal_speed) + jnp.sqrt(ratio_heat * press / dens)
    return (jnp.stack(rows, axis=0), wave_speed)


def rusanov(left_state, right_state, normal_axis):
    flux_left, speed_left = euler_flux(left_state, normal_axis)
    flux_right, speed_right = euler_flux(right_state, normal_axis)
    return 0.5 * (flux_left + flux_right) - 0.5 * jnp.maximum(speed_left, speed_right) * (
        right_state - left_state
    )


def conserve(density, velocity, pressure):
    energy = pressure / (ratio_heat - 1.0) + 0.5 * density * jnp.sum(velocity * velocity, axis=0)
    return jnp.concatenate([density[None], density[None] * velocity, energy[None]], axis=0)


def advance(padded, conserved):
    face_x = rusanov(padded[:, :-1], padded[:, 1:], 0)
    divergence = face_x[:, 1:] - face_x[:, :-1]
    face_y = rusanov(conserved, jnp.roll(conserved, -1, axis=2), 1)
    divergence = divergence + face_y - jnp.roll(face_y, 1, axis=2)
    mirror_sign = jnp.array([1.0, 1.0, 1.0, -1.0, 1.0], dtype=conserved.dtype)[:, None, None, None]
    padded_z = jnp.concatenate(
        [conserved[..., :1] * mirror_sign, conserved, conserved[..., -1:]], axis=3
    )
    face_z = rusanov(padded_z[..., :-1], padded_z[..., 1:], 2)
    divergence = divergence + face_z[..., 1:] - face_z[..., :-1]
    return conserved - step_ratio * divergence


def wall_pressure(state):
    bottom = state[..., 0]
    return (ratio_heat - 1.0) * (
        bottom[4] - 0.5 * jnp.sum(bottom[1:4] * bottom[1:4], axis=0) / bottom[0]
    )


def wall_at_kernel(wall_ref, index_ref, out_ref):
    index = index_ref[...]
    lanes = index.shape[1]
    low = index % lanes
    result = jnp.zeros(index.shape, jnp.float32)
    for row in range(wall_ref.shape[0]):
        source = jnp.broadcast_to(wall_ref[row : row + 1, :], index.shape)
        found = jnp.take_along_axis(source, low, axis=1)
        result = jnp.where(index // lanes == row, found, result)
    out_ref[...] = result


def wall_at(wall_row, correlation):
    lanes = correlation.shape[1]
    rows = -(-wall_row.shape[0] // lanes)
    table = jnp.pad(wall_row, (0, rows * lanes - wall_row.shape[0])).reshape(rows, lanes)
    return pl.pallas_call(
        wall_at_kernel, out_shape=jax.ShapeDtypeStruct(correlation.shape, jnp.float32)
    )(table, correlation)


def cho_apply(gram, projected):
    factor = jnp.linalg.cholesky(gram)
    middle = lax.linalg.triangular_solve(factor, projected[:, None], left_side=True, lower=True)
    return lax.linalg.triangular_solve(
        factor, middle, left_side=True, lower=True, transpose_a=True
    )[:, 0]


def on_device(
    density,
    velocity,
    pressure,
    rbf_blocks,
    correlation,
    normals,
    routes,
    targets,
    stiffness,
    coupling,
    inverse_diag,
    displacement,
    diff_res,
    diff_disp,
):
    conserved = conserve(density, velocity, pressure)
    padded = extended(conserved, ((("group", "dev"), 1),), 1)
    fluid_next = advance(padded, conserved)
    wall_row = wall_pressure(fluid_next).reshape(-1)
    weighted = (wall_at(wall_row, correlation)[:, None, :] * normals).astype(jnp.bfloat16)
    block_loads = jnp.einsum(
        "bci,bij->bcj", weighted, rbf_blocks, preferred_element_type=jnp.float32
    )
    blocks = block_loads.shape[0]
    width_row = block_loads.shape[1] * block_loads.shape[2]
    peer_count = lax.axis_size(("group", "dev"))
    capacity = max(2, 2 * blocks // peer_count)
    slot_count = peer_count * capacity
    target_dev = routes[:, 0]
    member = (target_dev[:, None] == jnp.arange(peer_count, dtype=jnp.int32)[None, :]).astype(
        jnp.int32
    )
    position = jnp.sum((jnp.cumsum(member, axis=0) - member) * member, axis=1)
    slot_id = target_dev * capacity + position
    send_loads = (
        jnp.zeros((slot_count, width_row), jnp.float32)
        .at[slot_id]
        .set(block_loads.reshape(blocks, width_row))
    )
    send_tag = (
        jnp.full((slot_count,), -1.0, jnp.float32).at[slot_id].set(targets.astype(jnp.float32))
    )
    got_loads, got_tag = (
        lax.all_to_all(
            send_loads.reshape(peer_count, capacity, width_row),
            ("group", "dev"),
            split_axis=0,
            concat_axis=0,
            tiled=True,
        ),
        lax.all_to_all(
            send_tag.reshape(peer_count, capacity),
            ("group", "dev"),
            split_axis=0,
            concat_axis=0,
            tiled=True,
        ),
    )
    got_loads = got_loads.reshape(slot_count, width_row)
    got_tag = got_tag.reshape(slot_count)
    solid_count = displacement.shape[0]
    selector = (got_tag[None, :] == jnp.arange(solid_count, dtype=jnp.float32)[:, None]).astype(
        jnp.float32
    )
    solid_load = jnp.dot(
        selector, got_loads, precision=lax.Precision.HIGHEST, preferred_element_type=jnp.float32
    ).reshape(displacement.shape)
    disp_half = displacement.astype(jnp.bfloat16)
    prior_block = shifted(disp_half[-1:], ("group", "dev"), 1)
    earlier = jnp.concatenate([prior_block, disp_half[:-1]], axis=0)
    solid_res = jnp.einsum("bcj,bij->bci", disp_half, stiffness, preferred_element_type=jnp.float32)
    solid_res = (
        solid_res
        + jnp.einsum("bcj,bij->bci", earlier, coupling, preferred_element_type=jnp.float32)
        - solid_load
    )
    coupling_res = -inverse_diag * solid_res
    projected_local = jnp.einsum(
        "mbcj,bcj->m", diff_res, coupling_res, precision=lax.Precision.HIGHEST
    )
    gram_local = jnp.einsum("mbcj,nbcj->mn", diff_res, diff_res, precision=lax.Precision.HIGHEST)
    columns = projected_local.shape[0]
    stats = jnp.concatenate([gram_local.reshape(-1), projected_local])
    everyone = lax.all_to_all(
        jnp.broadcast_to(stats[None], (peer_count, stats.shape[0])),
        ("group", "dev"),
        split_axis=0,
        concat_axis=0,
        tiled=True,
    )
    totals = jnp.sum(everyone, axis=0)
    gram_matrix = totals[: columns * columns].reshape(columns, columns)
    projected = totals[columns * columns :]
    mixing = -cho_apply(gram_matrix, projected)
    disp_next = (
        displacement
        + coupling_res
        + jnp.einsum("mbcj,m->bcj", diff_disp, mixing, precision=lax.Precision.HIGHEST)
    )
    reply_rows = disp_next.astype(jnp.bfloat16).reshape(solid_count, width_row)
    replies = jnp.dot(
        selector.T.astype(jnp.bfloat16), reply_rows, preferred_element_type=jnp.float32
    ).astype(jnp.bfloat16)
    returned = lax.all_to_all(
        replies.reshape(peer_count, capacity, width_row),
        ("group", "dev"),
        split_axis=0,
        concat_axis=0,
        tiled=True,
    )
    picked = returned.reshape(slot_count, width_row)[slot_id].reshape(block_loads.shape)
    wall_motion = jnp.einsum("bij,bcj->bci", rbf_blocks, picked, preferred_element_type=jnp.float32)
    return (fluid_next, disp_next, wall_motion)


def solution(mesh):
    placed = (
        P(("group", "dev"), None, None),
        P(None, ("group", "dev"), None, None),
        P(("group", "dev"), None, None),
        P(("group", "dev"), None, None),
        P(("group", "dev"), None),
        P(("group", "dev"), None, None),
        P(("group", "dev"), None),
        P(("group", "dev")),
        P(("group", "dev"), None, None),
        P(("group", "dev"), None, None),
        P(("group", "dev"), None, None),
        P(("group", "dev"), None, None),
        P(None, ("group", "dev"), None, None),
        P(None, ("group", "dev"), None, None),
    )
    return jax.shard_map(
        on_device,
        mesh=mesh,
        in_specs=placed,
        out_specs=(
            P(None, ("group", "dev"), None, None),
            P(("group", "dev"), None, None),
            P(("group", "dev"), None, None),
        ),
        check_vma=False,
    )
```

```python
import functools

import jax
import jax.numpy as jnp
from jax import lax
from jax.experimental import pallas as pl
from jax.experimental.pallas import tpu as pltpu
from jax.sharding import PartitionSpec as P

ratio_heat = 1.4
step_ratio = 0.03
AXES = ("group", "dev")
MESH = pl.DeviceIdType.MESH
LAST = (((1,), (1,)), ((), ()))


def conserve(prim):
    dens, u, v, w, press = prim
    energy = press / (ratio_heat - 1.0) + 0.5 * dens * (u * u + v * v + w * w)
    return (dens, dens * u, dens * v, dens * w, energy)


def flux_parts(prim, axis):
    state = conserve(prim)
    normal = prim[1 + axis]
    press = prim[4]
    rows = [row * normal for row in state]
    rows[1 + axis] = rows[1 + axis] + press
    rows[4] = rows[4] + press * normal
    speed = jnp.abs(normal) + jnp.sqrt(ratio_heat * press / prim[0])
    return state, rows, speed


def face_difference(low, mid, high, axis):
    state_l, flux_l, speed_l = flux_parts(low, axis)
    state_m, _, speed_m = flux_parts(mid, axis)
    state_h, flux_h, speed_h = flux_parts(high, axis)
    upper = jnp.maximum(speed_m, speed_h)
    lower = jnp.maximum(speed_l, speed_m)
    return [
        0.5 * (fh - fl) - 0.5 * (upper * (sh - sm) - lower * (sm - sl))
        for fh, fl, sh, sm, sl in zip(flux_h, flux_l, state_h, state_m, state_l)
    ]


def advance(mid, x_pair, y_pair, z_pair):
    div_x = face_difference(x_pair[0], mid, x_pair[1], 0)
    div_y = face_difference(y_pair[0], mid, y_pair[1], 1)
    div_z = face_difference(z_pair[0], mid, z_pair[1], 2)
    return [
        row - step_ratio * (a + b + c)
        for row, a, b, c in zip(conserve(mid), div_x, div_y, div_z)
    ]


def flow_kernel(dens_ref, vel_ref, press_ref, low_ref, high_ref, out_ref):
    height, lanes = dens_ref.shape[1:]
    chunk = next(c for c in (32, 16, 8, height) if height % c == 0)
    row = lax.broadcasted_iota(jnp.int32, (chunk, lanes), 0)
    lane = lax.broadcasted_iota(jnp.int32, (chunk, lanes), 1)
    fields = [dens_ref.at[0]] + [vel_ref.at[i, 0] for i in range(3)] + [press_ref.at[0]]
    for start in range(0, height, chunk):
        rows = slice(start, start + chunk)
        before = (start - 1) % height
        after = (start + chunk) % height
        mid = [f[rows, :] for f in fields]
        y_low = [
            jnp.where(row == 0, f[before : before + 1, :], pltpu.roll(m, 1, 0))
            for f, m in zip(fields, mid)
        ]
        y_high = [
            jnp.where(row == chunk - 1, f[after : after + 1, :], pltpu.roll(m, chunk - 1, 0))
            for f, m in zip(fields, mid)
        ]
        signs = (1.0, 1.0, 1.0, -1.0, 1.0)
        z_low = [jnp.where(lane == 0, s * m, pltpu.roll(m, 1, 1)) for s, m in zip(signs, mid)]
        z_high = [jnp.where(lane == lanes - 1, m, pltpu.roll(m, lanes - 1, 1)) for m in mid]
        x_low = [low_ref[i, rows, :].astype(jnp.float32) for i in range(5)]
        x_high = [high_ref[i, rows, :].astype(jnp.float32) for i in range(5)]
        result = advance(mid, (x_low, x_high), (y_low, y_high), (z_low, z_high))
        for i in range(5):
            out_ref[i, 0, rows, :] = result[i]


def thirds(value):
    high = value.astype(jnp.bfloat16)
    rest = value - high.astype(jnp.float32)
    middle = rest.astype(jnp.bfloat16)
    low = (rest - middle.astype(jnp.float32)).astype(jnp.bfloat16)
    return high, middle, low


def select_rows(chooser, value):
    parts = [
        jnp.dot(chooser, part, preferred_element_type=jnp.float32) for part in thirds(value)
    ]
    return (parts[2] + parts[1]) + parts[0]


def couple_kernel(
    peers,
    width,
    wall_ref,
    prim_ref,
    normals_ref,
    index_ref,
    rbf_ref,
    pick_ref,
    place_ref,
    tags_ref,
    stiff_ref,
    coup_ref,
    inv_ref,
    disp_ref,
    res_ref,
    dif_ref,
    low_ref,
    high_ref,
    next_ref,
    motion_ref,
    side_ref,
    prior_ref,
    tag_in,
    load_out,
    load_in,
    reply_out,
    reply_in,
    stat_out,
    stat_in,
    loads,
    slots,
    solid,
    products,
    near_send,
    near_recv,
    tag_send,
    tag_recv,
    load_send,
    load_recv,
    stat_send,
    stat_recv,
    reply_send,
    reply_recv,
):
    me = lax.axis_index("group") * width + lax.axis_index("dev")
    blocks = index_ref.shape[0]
    count = disp_ref.shape[0]
    columns = res_ref.shape[0]
    capacity = tags_ref.shape[1]
    nodes = index_ref.shape[1]

    def place(peer):
        return (peer // width, peer % width)

    def hop(distance):
        return (me + distance) % peers

    barrier = pltpu.get_barrier_semaphore()

    def greet(step, carry):
        pl.semaphore_signal(barrier, inc=1, device_id=place(hop(step)), device_id_type=MESH)
        return carry

    lax.fori_loop(1, peers, greet, 0)
    pl.semaphore_wait(barrier, peers - 1)

    def near(slot, src, dst, distance):
        return pltpu.make_async_remote_copy(
            src_ref=src,
            dst_ref=dst,
            send_sem=near_send.at[slot],
            recv_sem=near_recv.at[slot],
            device_id=place(hop(distance)),
            device_id_type=MESH,
        )

    wall_up = near(0, wall_ref.at[0], side_ref.at[0], 1)
    wall_down = near(1, wall_ref.at[0], side_ref.at[1], peers - 1)
    prior = near(2, disp_ref.at[count - 1], prior_ref, 1)
    bulk_up = near(3, prim_ref, low_ref, 1)
    bulk_down = near(4, prim_ref, high_ref, peers - 1)

    def spread(src, dst, send, recv, indexed):
        def begin(step, carry):
            peer = hop(step)
            pltpu.make_async_remote_copy(
                src_ref=src.at[peer] if indexed else src,
                dst_ref=dst.at[me],
                send_sem=send.at[step],
                recv_sem=recv.at[step],
                device_id=place(peer),
                device_id_type=MESH,
            ).start()
            return carry

        lax.fori_loop(1, peers, begin, 0)

    def gather(src, dst, send, recv, indexed):
        def finish(step, carry):
            pltpu.make_async_remote_copy(
                src_ref=src.at[hop(step)] if indexed else src,
                dst_ref=dst.at[hop(peers - step)],
                send_sem=send.at[step],
                recv_sem=recv.at[step],
                device_id=place(hop(step)),
                device_id_type=MESH,
            ).wait()
            return carry

        lax.fori_loop(1, peers, finish, 0)

    wall_up.start()
    wall_down.start()
    prior.start()
    spread(tags_ref, tag_in, tag_send, tag_recv, True)
    bulk_up.start()
    bulk_down.start()
    tag_in[me] = tags_ref[me]

    products[...] = jnp.zeros_like(products)
    for m in range(columns):
        for n in range(m, columns):
            line = jnp.sum(jnp.sum(res_ref[m] * res_ref[n], axis=0), axis=0, keepdims=True)
            products[m * columns + n : m * columns + n + 1, :] = line
            products[n * columns + m : n * columns + m + 1, :] = line

    wall_up.wait()
    wall_down.wait()

    def variant(i):
        return [wall_ref[i, k : k + 1, :] for k in range(5)]

    mid = variant(0)
    mirror = list(mid)
    mirror[3] = -mirror[3]
    beside = [[side_ref[j, k : k + 1, :] for k in range(5)] for j in range(2)]
    bottom = advance(mid, beside, (variant(3), variant(2)), (mirror, variant(1)))
    kinetic = bottom[1] * bottom[1] + bottom[2] * bottom[2] + bottom[3] * bottom[3]
    wall = (ratio_heat - 1.0) * (bottom[4] - 0.5 * kinetic / bottom[0])

    index = index_ref[...]
    low = index % nodes
    found = jnp.zeros(index.shape, jnp.float32)
    for part in range(wall.shape[1] // nodes):
        source = jnp.broadcast_to(wall[:, part * nodes : (part + 1) * nodes], index.shape)
        taken = jnp.take_along_axis(source, low, axis=1)
        found = jnp.where(index // nodes == part, taken, found)
    slots[0:blocks, 0:nodes] = found
    for b in range(blocks):
        weighted = (slots[b : b + 1, 0:nodes] * normals_ref[b]).astype(jnp.bfloat16)
        loads[b, 0:3, :] = jnp.dot(weighted, rbf_ref[b], preferred_element_type=jnp.float32)
    spans = [slice(c * nodes, (c + 1) * nodes) for c in range(3)]
    for c in range(3):
        slots[:, spans[c]] = select_rows(place_ref[...], loads[:, c, :])
    for p in range(peers):
        load_out[p] = slots[p * capacity : (p + 1) * capacity, :]
    spread(load_out, load_in, load_send, load_recv, True)
    load_in[me] = load_out[me]

    prior.wait()
    first = (me > 0).astype(jnp.float32)
    for t in range(count):
        half = disp_ref[t].astype(jnp.bfloat16)
        earlier = disp_ref[t - 1] if t else prior_ref[...] * first
        part = lax.dot_general(half, stiff_ref[t], LAST, preferred_element_type=jnp.float32)
        part = part + lax.dot_general(
            earlier.astype(jnp.bfloat16), coup_ref[t], LAST, preferred_element_type=jnp.float32
        )
        solid[t, 0:3, :] = part

    gather(tags_ref, tag_in, tag_send, tag_recv, True)
    for p in range(peers):
        slots[p * capacity : (p + 1) * capacity, spans[0]] = tag_in[p]
    tags = slots[:, spans[0]]
    lane = lax.broadcasted_iota(jnp.int32, tags.shape, 1).astype(jnp.float32)
    chooser = (tags == lane).astype(jnp.float32)[:, 0:count].astype(jnp.bfloat16)
    turned = tags.T[0:count, :]
    line_id = lax.broadcasted_iota(jnp.int32, turned.shape, 0).astype(jnp.float32)
    collector = (turned == line_id).astype(jnp.float32).astype(jnp.bfloat16)

    gather(load_out, load_in, load_send, load_recv, True)
    for p in range(peers):
        slots[p * capacity : (p + 1) * capacity, :] = load_in[p]
    for c in range(3):
        solid[:, c, :] = solid[:, c, :] - select_rows(collector, slots[:, spans[c]])
    change = -inv_ref[...] * solid[:, 0:3, :]
    for m in range(columns):
        line = jnp.sum(jnp.sum(res_ref[m] * change, axis=0), axis=0, keepdims=True)
        at = columns * columns + m
        products[at : at + 1, :] = line
    stat_out[...] = jnp.sum(products[...].T, axis=0, keepdims=True)
    spread(stat_out, stat_in, stat_send, stat_recv, False)
    stat_in[me] = stat_out[...]
    solid[:, 0:3, :] = disp_ref[...] + change
    gather(stat_out, stat_in, stat_send, stat_recv, False)
    total = jnp.sum(stat_in[...], axis=0)
    shape = (columns, nodes)
    m_id = lax.broadcasted_iota(jnp.int32, shape, 0)
    n_id = lax.broadcasted_iota(jnp.int32, shape, 1)
    source = jnp.where(
        n_id < columns, m_id * columns + n_id, columns * columns + m_id
    )
    matrix = jnp.take_along_axis(jnp.broadcast_to(total, shape), source, axis=1)
    for k in range(columns):
        line = matrix[k : k + 1, :]
        scaled = line / matrix[k : k + 1, k : k + 1]
        matrix = jnp.where(m_id == k, scaled, matrix - matrix[:, k : k + 1] * scaled)
    mixing = -matrix[:, columns : columns + 1]
    result = solid[:, 0:3, :]
    for m in range(columns):
        result = result + dif_ref[m] * mixing[m : m + 1, :].reshape(1, 1, 1)
    next_ref[...] = result
    solid[:, 0:3, :] = result
    for c in range(3):
        rows = solid[:, c, :].astype(jnp.bfloat16)
        slots[:, spans[c]] = jnp.dot(chooser, rows, preferred_element_type=jnp.float32)
    for p in range(peers):
        reply_out[p] = slots[p * capacity : (p + 1) * capacity, :].astype(jnp.bfloat16)
    spread(reply_out, reply_in, reply_send, reply_recv, True)
    reply_in[me] = reply_out[me]
    gather(reply_out, reply_in, reply_send, reply_recv, True)
    for p in range(peers):
        slots[p * capacity : (p + 1) * capacity, :] = reply_in[p].astype(jnp.float32)
    for c in range(3):
        rows = slots[:, spans[c]].astype(jnp.bfloat16)
        loads[:, c, :] = jnp.dot(pick_ref[...], rows, preferred_element_type=jnp.float32)
    for b in range(blocks):
        reply = loads[b, 0:3, :].astype(jnp.bfloat16)
        motion_ref[b] = lax.dot_general(
            reply, rbf_ref[b], LAST, preferred_element_type=jnp.float32
        )
    bulk_up.wait()
    bulk_down.wait()


def on_device(
    density,
    velocity,
    pressure,
    rbf_blocks,
    correlation,
    normals,
    routes,
    targets,
    stiffness,
    coupling,
    inverse_diag,
    displacement,
    diff_res,
    diff_disp,
):
    f32, bf16 = jnp.float32, jnp.bfloat16
    width = lax.axis_size("dev")
    peers = lax.axis_size(AXES)
    blocks, nodes = correlation.shape
    count = displacement.shape[0]
    columns = diff_res.shape[0]
    height, depth = density.shape[1:]
    capacity = max(2, 2 * blocks // peers)
    slot_count = peers * capacity

    ends = jnp.concatenate([density[None], velocity, pressure[None]], axis=0)[:, 0, :, 0:2]
    ends = jnp.transpose(ends, (2, 0, 1))
    ends = jnp.stack(
        [ends[0], ends[1], jnp.roll(ends[0], -1, axis=1), jnp.roll(ends[0], 1, axis=1)]
    )
    padded = -(-height // nodes) * nodes
    ends = jnp.pad(ends, ((0, 0), (0, 3), (0, padded - height)), constant_values=1.0)
    prim = jnp.concatenate([density, velocity[:, 0], pressure], axis=0).astype(bf16)

    owner = routes[:, 0]
    same = (owner[:, None] == owner[None, :]) & (
        jnp.arange(blocks)[:, None] > jnp.arange(blocks)[None, :]
    )
    slot_id = owner * capacity + jnp.sum(same.astype(jnp.int32), axis=1)
    chosen = slot_id[:, None] == jnp.arange(slot_count, dtype=jnp.int32)[None, :]
    pick = chosen.astype(bf16)
    put = (jnp.arange(slot_count, dtype=jnp.int32)[:, None] == slot_id[None, :])
    tag = jnp.sum(jnp.where(chosen, targets[:, None] + 1, 0), axis=0) - 1
    tags = jnp.broadcast_to(
        tag.astype(f32).reshape(peers, capacity)[:, :, None], (peers, capacity, nodes)
    )

    vmem = pl.BlockSpec(memory_space=pltpu.VMEM)
    anywhere = pl.BlockSpec(memory_space=pl.ANY)
    dma = pltpu.SemaphoreType.DMA
    halo = jax.ShapeDtypeStruct((5, height, depth), bf16)
    width_row = 3 * nodes
    low, high, disp_next, wall_motion = pl.pallas_call(
        functools.partial(couple_kernel, peers, width),
        out_shape=(
            halo,
            halo,
            jax.ShapeDtypeStruct(displacement.shape, f32),
            jax.ShapeDtypeStruct(normals.shape, f32),
        ),
        in_specs=[vmem, anywhere] + [vmem] * 12,
        out_specs=(anywhere, anywhere, vmem, vmem),
        scratch_shapes=[
            pltpu.VMEM((2, 8, padded), f32),
            pltpu.VMEM((3, nodes), f32),
            pltpu.VMEM((peers, capacity, nodes), f32),
            pltpu.VMEM((peers, capacity, width_row), f32),
            pltpu.VMEM((peers, capacity, width_row), f32),
            pltpu.VMEM((peers, capacity, width_row), bf16),
            pltpu.VMEM((peers, capacity, width_row), bf16),
            pltpu.VMEM((1, nodes), f32),
            pltpu.VMEM((peers, 1, nodes), f32),
            pltpu.VMEM((blocks, 8, nodes), f32),
            pltpu.VMEM((slot_count, width_row), f32),
            pltpu.VMEM((count, 8, nodes), f32),
            pltpu.VMEM((nodes, nodes), f32),
            dma((5,)),
            dma((5,)),
        ]
        + [dma((peers,))] * 8,
        compiler_params=pltpu.CompilerParams(collective_id=0, has_side_effects=True),
    )(
        ends,
        prim,
        normals,
        correlation,
        rbf_blocks,
        pick,
        put.astype(bf16),
        tags,
        stiffness,
        coupling,
        inverse_diag,
        displacement,
        diff_res,
        diff_disp,
    )
    fluid_next = pl.pallas_call(
        flow_kernel,
        out_shape=jax.ShapeDtypeStruct((5,) + density.shape, f32),
        in_specs=[vmem] * 5,
        out_specs=vmem,
    )(density, velocity, pressure, low, high)
    return (fluid_next, disp_next, wall_motion)


def solution(mesh):
    placed = (
        P(("group", "dev"), None, None),
        P(None, ("group", "dev"), None, None),
        P(("group", "dev"), None, None),
        P(("group", "dev"), None, None),
        P(("group", "dev"), None),
        P(("group", "dev"), None, None),
        P(("group", "dev"), None),
        P(("group", "dev")),
        P(("group", "dev"), None, None),
        P(("group", "dev"), None, None),
        P(("group", "dev"), None, None),
        P(("group", "dev"), None, None),
        P(None, ("group", "dev"), None, None),
        P(None, ("group", "dev"), None, None),
    )
    return jax.shard_map(
        on_device,
        mesh=mesh,
        in_specs=placed,
        out_specs=(
            P(None, ("group", "dev"), None, None),
            P(("group", "dev"), None, None),
            P(("group", "dev"), None, None),
        ),
        check_vma=False,
    )
```

```python
import functools

import jax
import jax.numpy as jnp
from jax import lax
from jax.experimental import pallas as pl
from jax.experimental.pallas import tpu as pltpu
from jax.sharding import PartitionSpec as P

ratio_heat = 1.4
step_ratio = 0.03
AXES = ("group", "dev")
MESH = pl.DeviceIdType.MESH
LAST = (((1,), (1,)), ((), ()))


def conserve(prim):
    dens, u, v, w, press = prim
    energy = press / (ratio_heat - 1.0) + 0.5 * dens * (u * u + v * v + w * w)
    return (dens, dens * u, dens * v, dens * w, energy)


def flux_parts(prim, axis):
    state = conserve(prim)
    normal = prim[1 + axis]
    press = prim[4]
    rows = [row * normal for row in state]
    rows[1 + axis] = rows[1 + axis] + press
    rows[4] = rows[4] + press * normal
    speed = jnp.abs(normal) + jnp.sqrt(ratio_heat * press / prim[0])
    return state, rows, speed


def face_difference(low, mid, high, axis):
    state_l, flux_l, speed_l = flux_parts(low, axis)
    state_m, _, speed_m = flux_parts(mid, axis)
    state_h, flux_h, speed_h = flux_parts(high, axis)
    upper = jnp.maximum(speed_m, speed_h)
    lower = jnp.maximum(speed_l, speed_m)
    return [
        0.5 * (fh - fl) - 0.5 * (upper * (sh - sm) - lower * (sm - sl))
        for fh, fl, sh, sm, sl in zip(flux_h, flux_l, state_h, state_m, state_l)
    ]


def advance(mid, x_pair, y_pair, z_pair):
    div_x = face_difference(x_pair[0], mid, x_pair[1], 0)
    div_y = face_difference(y_pair[0], mid, y_pair[1], 1)
    div_z = face_difference(z_pair[0], mid, z_pair[1], 2)
    return [
        row - step_ratio * (a + b + c)
        for row, a, b, c in zip(conserve(mid), div_x, div_y, div_z)
    ]


def flow_kernel(dens_ref, vel_ref, press_ref, low_ref, high_ref, out_ref):
    height, lanes = dens_ref.shape[1:]
    chunk = next(c for c in (32, 16, 8, height) if height % c == 0)
    row = lax.broadcasted_iota(jnp.int32, (chunk, lanes), 0)
    lane = lax.broadcasted_iota(jnp.int32, (chunk, lanes), 1)
    fields = [dens_ref.at[0]] + [vel_ref.at[i, 0] for i in range(3)] + [press_ref.at[0]]
    for start in range(0, height, chunk):
        rows = slice(start, start + chunk)
        before = (start - 1) % height
        after = (start + chunk) % height
        mid = [f[rows, :] for f in fields]
        y_low = [
            jnp.where(row == 0, f[before : before + 1, :], pltpu.roll(m, 1, 0))
            for f, m in zip(fields, mid)
        ]
        y_high = [
            jnp.where(row == chunk - 1, f[after : after + 1, :], pltpu.roll(m, chunk - 1, 0))
            for f, m in zip(fields, mid)
        ]
        signs = (1.0, 1.0, 1.0, -1.0, 1.0)
        z_low = [jnp.where(lane == 0, s * m, pltpu.roll(m, 1, 1)) for s, m in zip(signs, mid)]
        z_high = [jnp.where(lane == lanes - 1, m, pltpu.roll(m, lanes - 1, 1)) for m in mid]
        x_low = [low_ref[i, rows, :].astype(jnp.float32) for i in range(5)]
        x_high = [high_ref[i, rows, :].astype(jnp.float32) for i in range(5)]
        result = advance(mid, (x_low, x_high), (y_low, y_high), (z_low, z_high))
        for i in range(5):
            out_ref[i, 0, rows, :] = result[i]


def prepare_kernel(
    capacity,
    dens_ref,
    vel_ref,
    press_ref,
    owner_ref,
    owner_row_ref,
    target_ref,
    ends_ref,
    prim_ref,
    pick_ref,
    place_ref,
    tags_ref,
    column,
):
    height, lanes = dens_ref.shape[1:]
    fields = [dens_ref.at[0]] + [vel_ref.at[i, 0] for i in range(3)] + [press_ref.at[0]]
    ends_ref[...] = jnp.ones_like(ends_ref)
    column[...] = jnp.ones_like(column)
    for i, field in enumerate(fields):
        value = field[...]
        prim_ref[i] = value.astype(jnp.bfloat16)
        column[0:height, :] = value
        for start in range(0, column.shape[0], lanes):
            turned = column[start : start + lanes, :].T
            for z in range(2):
                ends_ref[z, i : i + 1, start : start + lanes] = turned[z : z + 1, :]
    edge = ends_ref[0]
    total = edge.shape[1]
    lane = lax.broadcasted_iota(jnp.int32, edge.shape, 1)
    ends_ref[2] = jnp.where(lane == height - 1, edge[:, 0:1], pltpu.roll(edge, total - 1, 1))
    ends_ref[3] = jnp.where(lane == 0, edge[:, height - 1 : height], pltpu.roll(edge, 1, 1))

    blocks, slot_count = pick_ref.shape
    owner, owner_row = owner_ref[...], owner_row_ref[...]
    row_id = lax.broadcasted_iota(jnp.int32, (blocks, blocks), 0)
    column_id = lax.broadcasted_iota(jnp.int32, (blocks, blocks), 1)
    same = jnp.where(owner == owner_row, 1.0, 0.0)
    rank = jnp.sum(jnp.where(column_id < row_id, same, 0.0), axis=1, keepdims=True)
    rank_row = jnp.sum(jnp.where(row_id < column_id, same, 0.0), axis=0, keepdims=True)
    slot = owner.astype(jnp.float32) * capacity + rank
    slot_row = owner_row.astype(jnp.float32) * capacity + rank_row
    lane_id = lax.broadcasted_iota(jnp.int32, (blocks, slot_count), 1).astype(jnp.float32)
    pick_ref[...] = jnp.where(slot == lane_id, 1.0, 0.0).astype(jnp.bfloat16)
    line_id = lax.broadcasted_iota(jnp.int32, (slot_count, blocks), 0).astype(jnp.float32)
    placed = jnp.where(slot_row == line_id, 1.0, 0.0)
    place_ref[...] = placed.astype(jnp.bfloat16)
    tag = jnp.sum(placed * (target_ref[...].astype(jnp.float32) + 1.0), axis=1, keepdims=True)
    tag = jnp.broadcast_to(tag - 1.0, (slot_count, tags_ref.shape[2]))
    for p in range(tags_ref.shape[0]):
        tags_ref[p] = tag[p * capacity : (p + 1) * capacity, :]


def thirds(value):
    high = value.astype(jnp.bfloat16)
    rest = value - high.astype(jnp.float32)
    middle = rest.astype(jnp.bfloat16)
    low = (rest - middle.astype(jnp.float32)).astype(jnp.bfloat16)
    return high, middle, low


def select_rows(chooser, value):
    parts = [
        jnp.dot(chooser, part, preferred_element_type=jnp.float32) for part in thirds(value)
    ]
    return (parts[2] + parts[1]) + parts[0]


def couple_kernel(
    peers,
    width,
    wall_ref,
    prim_ref,
    normals_ref,
    index_ref,
    rbf_ref,
    pick_ref,
    place_ref,
    tags_ref,
    stiff_ref,
    coup_ref,
    inv_ref,
    disp_ref,
    res_ref,
    dif_ref,
    low_ref,
    high_ref,
    next_ref,
    motion_ref,
    side_ref,
    prior_ref,
    tag_in,
    load_out,
    load_in,
    reply_out,
    reply_in,
    stat_out,
    stat_in,
    loads,
    slots,
    solid,
    products,
    near_send,
    near_recv,
    tag_send,
    tag_recv,
    load_send,
    load_recv,
    stat_send,
    stat_recv,
    reply_send,
    reply_recv,
):
    me = lax.axis_index("group") * width + lax.axis_index("dev")
    blocks = index_ref.shape[0]
    count = disp_ref.shape[1]
    columns = res_ref.shape[0]
    capacity = tags_ref.shape[1]
    nodes = index_ref.shape[1]

    def place(peer):
        return (peer // width, peer % width)

    def hop(distance):
        return (me + distance) % peers

    barrier = pltpu.get_barrier_semaphore()

    def greet(step, carry):
        pl.semaphore_signal(barrier, inc=1, device_id=place(hop(step)), device_id_type=MESH)
        return carry

    lax.fori_loop(1, peers, greet, 0)
    products[...] = jnp.zeros_like(products)
    for m in range(columns):
        for n in range(m, columns):
            line = jnp.sum(jnp.sum(res_ref[m] * res_ref[n], axis=0), axis=0, keepdims=True)
            products[m * columns + n : m * columns + n + 1, :] = line
            products[n * columns + m : n * columns + m + 1, :] = line
    pl.semaphore_wait(barrier, peers - 1)

    def near(slot, src, dst, distance):
        return pltpu.make_async_remote_copy(
            src_ref=src,
            dst_ref=dst,
            send_sem=near_send.at[slot],
            recv_sem=near_recv.at[slot],
            device_id=place(hop(distance)),
            device_id_type=MESH,
        )

    wall_up = near(0, wall_ref.at[0], side_ref.at[0], 1)
    wall_down = near(1, wall_ref.at[0], side_ref.at[1], peers - 1)
    tail = prior_ref.shape[1]
    prior = near(2, disp_ref.at[:, pl.ds(count - tail, tail), :], prior_ref, 1)
    bulk_up = near(3, prim_ref, low_ref, 1)
    bulk_down = near(4, prim_ref, high_ref, peers - 1)

    def spread(src, dst, send, recv, indexed):
        def begin(step, carry):
            peer = hop(step)
            pltpu.make_async_remote_copy(
                src_ref=src.at[peer] if indexed else src,
                dst_ref=dst.at[me],
                send_sem=send.at[step],
                recv_sem=recv.at[step],
                device_id=place(peer),
                device_id_type=MESH,
            ).start()
            return carry

        lax.fori_loop(1, peers, begin, 0)

    def gather(src, dst, send, recv, indexed):
        def finish(step, carry):
            pltpu.make_async_remote_copy(
                src_ref=src.at[hop(step)] if indexed else src,
                dst_ref=dst.at[hop(peers - step)],
                send_sem=send.at[step],
                recv_sem=recv.at[step],
                device_id=place(hop(step)),
                device_id_type=MESH,
            ).wait()
            return carry

        lax.fori_loop(1, peers, finish, 0)

    wall_up.start()
    wall_down.start()
    prior.start()
    spread(tags_ref, tag_in, tag_send, tag_recv, True)
    tag_in[me] = tags_ref[me]

    wall_up.wait()
    wall_down.wait()

    def variant(i):
        return [wall_ref[i, k : k + 1, :] for k in range(5)]

    mid = variant(0)
    mirror = list(mid)
    mirror[3] = -mirror[3]
    beside = [[side_ref[j, k : k + 1, :] for k in range(5)] for j in range(2)]
    bottom = advance(mid, beside, (variant(3), variant(2)), (mirror, variant(1)))
    kinetic = bottom[1] * bottom[1] + bottom[2] * bottom[2] + bottom[3] * bottom[3]
    wall = (ratio_heat - 1.0) * (bottom[4] - 0.5 * kinetic / bottom[0])

    index = index_ref[...]
    low = index % nodes
    found = jnp.zeros(index.shape, jnp.float32)
    for part in range(wall.shape[1] // nodes):
        source = jnp.broadcast_to(wall[:, part * nodes : (part + 1) * nodes], index.shape)
        taken = jnp.take_along_axis(source, low, axis=1)
        found = jnp.where(index // nodes == part, taken, found)
    for c in range(3):
        loads[:, c, :] = found * normals_ref[c]
    for b in range(blocks):
        weighted = loads[b, 0:3, :].astype(jnp.bfloat16)
        loads[b, 0:3, :] = jnp.dot(weighted, rbf_ref[b], preferred_element_type=jnp.float32)
    spans = [slice(c * nodes, (c + 1) * nodes) for c in range(3)]
    for c in range(3):
        slots[:, spans[c]] = select_rows(place_ref[...], loads[:, c, :])
    for p in range(peers):
        load_out[p] = slots[p * capacity : (p + 1) * capacity, :]
    spread(load_out, load_in, load_send, load_recv, True)
    bulk_up.start()
    bulk_down.start()
    load_in[me] = load_out[me]

    prior.wait()
    first = (me > 0).astype(jnp.float32)
    for c in range(3):
        solid[:, c, :] = disp_ref[c]
    for t in range(count - 1, -1, -1):
        half = solid[t, 0:3, :].astype(jnp.bfloat16)
        earlier = solid[t - 1, 0:3, :] if t else prior_ref[:, tail - 1, :] * first
        part = lax.dot_general(half, stiff_ref[t], LAST, preferred_element_type=jnp.float32)
        part = part + lax.dot_general(
            earlier.astype(jnp.bfloat16), coup_ref[t], LAST, preferred_element_type=jnp.float32
        )
        solid[t, 0:3, :] = part

    gather(tags_ref, tag_in, tag_send, tag_recv, True)
    for p in range(peers):
        slots[p * capacity : (p + 1) * capacity, spans[0]] = tag_in[p]
    tags = slots[:, spans[0]]
    lane = lax.broadcasted_iota(jnp.int32, tags.shape, 1).astype(jnp.float32)
    chooser = (tags == lane).astype(jnp.float32)[:, 0:count].astype(jnp.bfloat16)
    turned = tags.T[0:count, :]
    line_id = lax.broadcasted_iota(jnp.int32, turned.shape, 0).astype(jnp.float32)
    collector = (turned == line_id).astype(jnp.float32).astype(jnp.bfloat16)

    gather(load_out, load_in, load_send, load_recv, True)
    for p in range(peers):
        slots[p * capacity : (p + 1) * capacity, :] = load_in[p]
    change = [
        -inv_ref[c] * (solid[:, c, :] - select_rows(collector, slots[:, spans[c]]))
        for c in range(3)
    ]
    for m in range(columns):
        line = sum(res_ref[m, c] * change[c] for c in range(3))
        at = columns * columns + m
        products[at : at + 1, :] = jnp.sum(line, axis=0, keepdims=True)
    stat_out[...] = jnp.sum(products[...].T, axis=0, keepdims=True)
    spread(stat_out, stat_in, stat_send, stat_recv, False)
    stat_in[me] = stat_out[...]
    for c in range(3):
        next_ref[c] = disp_ref[c] + change[c]
    gather(stat_out, stat_in, stat_send, stat_recv, False)
    total = jnp.sum(stat_in[...], axis=0)
    shape = (columns, nodes)
    m_id = lax.broadcasted_iota(jnp.int32, shape, 0)
    n_id = lax.broadcasted_iota(jnp.int32, shape, 1)
    source = jnp.where(
        n_id < columns, m_id * columns + n_id, columns * columns + m_id
    )
    matrix = jnp.take_along_axis(jnp.broadcast_to(total, shape), source, axis=1)
    for k in range(columns):
        line = matrix[k : k + 1, :]
        scaled = line / matrix[k : k + 1, k : k + 1]
        matrix = jnp.where(m_id == k, scaled, matrix - matrix[:, k : k + 1] * scaled)
    mixing = -matrix[:, columns : columns + 1]
    for c in range(3):
        result = next_ref[c]
        for m in range(columns):
            result = result + dif_ref[m, c] * mixing[m : m + 1, :]
        next_ref[c] = result
        slots[:, spans[c]] = jnp.dot(
            chooser, result.astype(jnp.bfloat16), preferred_element_type=jnp.float32
        )
    for p in range(peers):
        reply_out[p] = slots[p * capacity : (p + 1) * capacity, :].astype(jnp.bfloat16)
    spread(reply_out, reply_in, reply_send, reply_recv, True)
    reply_in[me] = reply_out[me]
    gather(reply_out, reply_in, reply_send, reply_recv, True)
    for p in range(peers):
        slots[p * capacity : (p + 1) * capacity, :] = reply_in[p].astype(jnp.float32)
    for c in range(3):
        rows = slots[:, spans[c]].astype(jnp.bfloat16)
        loads[:, c, :] = jnp.dot(pick_ref[...], rows, preferred_element_type=jnp.float32)
    for b in range(blocks):
        reply = loads[b, 0:3, :].astype(jnp.bfloat16)
        loads[b, 0:3, :] = lax.dot_general(
            reply, rbf_ref[b], LAST, preferred_element_type=jnp.float32
        )
    for c in range(3):
        motion_ref[c] = loads[:, c, :]
    bulk_up.wait()
    bulk_down.wait()


def rows_last(value):
    return jnp.swapaxes(value, -3, -2)


def on_device(
    density,
    velocity,
    pressure,
    rbf_blocks,
    correlation,
    normals,
    routes,
    targets,
    stiffness,
    coupling,
    inverse_diag,
    displacement,
    diff_res,
    diff_disp,
):
    f32, bf16 = jnp.float32, jnp.bfloat16
    width = lax.axis_size("dev")
    peers = lax.axis_size(AXES)
    blocks, nodes = correlation.shape
    count = displacement.shape[0]
    columns = diff_res.shape[0]
    height, depth = density.shape[1:]
    capacity = max(2, 2 * blocks // peers)
    slot_count = peers * capacity

    padded = -(-height // depth) * depth
    halo = jax.ShapeDtypeStruct((5, height, depth), bf16)
    vmem = pl.BlockSpec(memory_space=pltpu.VMEM)
    anywhere = pl.BlockSpec(memory_space=pl.ANY)
    dma = pltpu.SemaphoreType.DMA
    ends, prim, pick, put, tags = pl.pallas_call(
        functools.partial(prepare_kernel, capacity),
        out_shape=(
            jax.ShapeDtypeStruct((4, 8, padded), f32),
            halo,
            jax.ShapeDtypeStruct((blocks, slot_count), bf16),
            jax.ShapeDtypeStruct((slot_count, blocks), bf16),
            jax.ShapeDtypeStruct((peers, capacity, nodes), f32),
        ),
        in_specs=[vmem] * 6,
        out_specs=(vmem,) * 5,
        scratch_shapes=[pltpu.VMEM((padded, depth), f32)],
    )(density, velocity, pressure, routes, routes.reshape(1, blocks), targets.reshape(1, blocks))
    width_row = 3 * nodes
    low, high, disp_next, wall_motion = pl.pallas_call(
        functools.partial(couple_kernel, peers, width),
        out_shape=(
            halo,
            halo,
            jax.ShapeDtypeStruct((3, count, nodes), f32),
            jax.ShapeDtypeStruct((3, blocks, nodes), f32),
        ),
        in_specs=[vmem, anywhere] + [vmem] * 12,
        out_specs=(anywhere, anywhere, vmem, vmem),
        scratch_shapes=[
            pltpu.VMEM((2, 8, padded), f32),
            pltpu.VMEM((3, 8, nodes), f32),
            pltpu.VMEM((peers, capacity, nodes), f32),
            pltpu.VMEM((peers, capacity, width_row), f32),
            pltpu.VMEM((peers, capacity, width_row), f32),
            pltpu.VMEM((peers, capacity, width_row), bf16),
            pltpu.VMEM((peers, capacity, width_row), bf16),
            pltpu.VMEM((1, nodes), f32),
            pltpu.VMEM((peers, 1, nodes), f32),
            pltpu.VMEM((blocks, 8, nodes), f32),
            pltpu.VMEM((slot_count, width_row), f32),
            pltpu.VMEM((count, 8, nodes), f32),
            pltpu.VMEM((nodes, nodes), f32),
            dma((5,)),
            dma((5,)),
        ]
        + [dma((peers,))] * 8,
        compiler_params=pltpu.CompilerParams(collective_id=0, has_side_effects=True),
    )(
        ends,
        prim,
        rows_last(normals),
        correlation,
        rbf_blocks,
        pick,
        put,
        tags,
        stiffness,
        coupling,
        rows_last(inverse_diag),
        rows_last(displacement),
        rows_last(diff_res),
        rows_last(diff_disp),
    )
    fluid_next = pl.pallas_call(
        flow_kernel,
        out_shape=jax.ShapeDtypeStruct((5,) + density.shape, f32),
        in_specs=[vmem] * 5,
        out_specs=vmem,
    )(density, velocity, pressure, low, high)
    return (fluid_next, rows_last(disp_next), rows_last(wall_motion))


def solution(mesh):
    placed = (
        P(("group", "dev"), None, None),
        P(None, ("group", "dev"), None, None),
        P(("group", "dev"), None, None),
        P(("group", "dev"), None, None),
        P(("group", "dev"), None),
        P(("group", "dev"), None, None),
        P(("group", "dev"), None),
        P(("group", "dev")),
        P(("group", "dev"), None, None),
        P(("group", "dev"), None, None),
        P(("group", "dev"), None, None),
        P(("group", "dev"), None, None),
        P(None, ("group", "dev"), None, None),
        P(None, ("group", "dev"), None, None),
    )
    return jax.shard_map(
        on_device,
        mesh=mesh,
        in_specs=placed,
        out_specs=(
            P(None, ("group", "dev"), None, None),
            P(("group", "dev"), None, None),
            P(("group", "dev"), None, None),
        ),
        check_vma=False,
    )
```

```python
import functools

import jax
import jax.numpy as jnp
from jax import lax
from jax.experimental import pallas as pl
from jax.experimental.pallas import tpu as pltpu
from jax.sharding import PartitionSpec as P

ratio_heat = 1.4
step_ratio = 0.03
AXES = ("group", "dev")
MESH = pl.DeviceIdType.MESH
LAST = (((1,), (1,)), ((), ()))


def conserve(prim):
    dens, u, v, w, press = prim
    energy = press / (ratio_heat - 1.0) + 0.5 * dens * (u * u + v * v + w * w)
    return (dens, dens * u, dens * v, dens * w, energy)


def flux_parts(prim, axis):
    state = conserve(prim)
    normal = prim[1 + axis]
    press = prim[4]
    rows = [row * normal for row in state]
    rows[1 + axis] = rows[1 + axis] + press
    rows[4] = rows[4] + press * normal
    speed = jnp.abs(normal) + jnp.sqrt(ratio_heat * press / prim[0])
    return state, rows, speed


def face_difference(low, mid, high, axis):
    state_l, flux_l, speed_l = flux_parts(low, axis)
    state_m, _, speed_m = flux_parts(mid, axis)
    state_h, flux_h, speed_h = flux_parts(high, axis)
    upper = jnp.maximum(speed_m, speed_h)
    lower = jnp.maximum(speed_l, speed_m)
    return [
        0.5 * (fh - fl) - 0.5 * (upper * (sh - sm) - lower * (sm - sl))
        for fh, fl, sh, sm, sl in zip(flux_h, flux_l, state_h, state_m, state_l)
    ]


def advance(mid, x_pair, y_pair, z_pair):
    div_x = face_difference(x_pair[0], mid, x_pair[1], 0)
    div_y = face_difference(y_pair[0], mid, y_pair[1], 1)
    div_z = face_difference(z_pair[0], mid, z_pair[1], 2)
    return [
        row - step_ratio * (a + b + c)
        for row, a, b, c in zip(conserve(mid), div_x, div_y, div_z)
    ]


def flow_kernel(dens_ref, vel_ref, press_ref, low_ref, high_ref, out_ref):
    height, lanes = dens_ref.shape[1:]
    chunk = next(c for c in (32, 16, 8, height) if height % c == 0)
    row = lax.broadcasted_iota(jnp.int32, (chunk, lanes), 0)
    lane = lax.broadcasted_iota(jnp.int32, (chunk, lanes), 1)
    fields = [dens_ref.at[0]] + [vel_ref.at[i, 0] for i in range(3)] + [press_ref.at[0]]
    for start in range(0, height, chunk):
        rows = slice(start, start + chunk)
        before = (start - 1) % height
        after = (start + chunk) % height
        mid = [f[rows, :] for f in fields]
        y_low = [
            jnp.where(row == 0, f[before : before + 1, :], pltpu.roll(m, 1, 0))
            for f, m in zip(fields, mid)
        ]
        y_high = [
            jnp.where(row == chunk - 1, f[after : after + 1, :], pltpu.roll(m, chunk - 1, 0))
            for f, m in zip(fields, mid)
        ]
        signs = (1.0, 1.0, 1.0, -1.0, 1.0)
        z_low = [jnp.where(lane == 0, s * m, pltpu.roll(m, 1, 1)) for s, m in zip(signs, mid)]
        z_high = [jnp.where(lane == lanes - 1, m, pltpu.roll(m, lanes - 1, 1)) for m in mid]
        x_low = [low_ref[i, rows, :].astype(jnp.float32) for i in range(5)]
        x_high = [high_ref[i, rows, :].astype(jnp.float32) for i in range(5)]
        result = advance(mid, (x_low, x_high), (y_low, y_high), (z_low, z_high))
        for i in range(5):
            out_ref[i, 0, rows, :] = result[i]


def prepare_kernel(
    capacity,
    dens_ref,
    vel_ref,
    press_ref,
    owner_ref,
    owner_row_ref,
    target_ref,
    ends_ref,
    prim_ref,
    pick_ref,
    place_ref,
    tags_ref,
    column,
):
    height, lanes = dens_ref.shape[1:]
    fields = [dens_ref.at[0]] + [vel_ref.at[i, 0] for i in range(3)] + [press_ref.at[0]]
    ends_ref[...] = jnp.ones_like(ends_ref)
    column[...] = jnp.ones_like(column)
    for i, field in enumerate(fields):
        value = field[...]
        prim_ref[i] = value.astype(jnp.bfloat16)
        column[0:height, :] = value
        for start in range(0, column.shape[0], lanes):
            turned = column[start : start + lanes, :].T
            for z in range(2):
                ends_ref[z, i : i + 1, start : start + lanes] = turned[z : z + 1, :]
    edge = ends_ref[0]
    total = edge.shape[1]
    lane = lax.broadcasted_iota(jnp.int32, edge.shape, 1)
    ends_ref[2] = jnp.where(lane == height - 1, edge[:, 0:1], pltpu.roll(edge, total - 1, 1))
    ends_ref[3] = jnp.where(lane == 0, edge[:, height - 1 : height], pltpu.roll(edge, 1, 1))

    blocks, slot_count = pick_ref.shape
    owner, owner_row = owner_ref[...], owner_row_ref[...]
    row_id = lax.broadcasted_iota(jnp.int32, (blocks, blocks), 0)
    column_id = lax.broadcasted_iota(jnp.int32, (blocks, blocks), 1)
    same = jnp.where(owner == owner_row, 1.0, 0.0)
    rank = jnp.sum(jnp.where(column_id < row_id, same, 0.0), axis=1, keepdims=True)
    rank_row = jnp.sum(jnp.where(row_id < column_id, same, 0.0), axis=0, keepdims=True)
    slot = owner.astype(jnp.float32) * capacity + rank
    slot_row = owner_row.astype(jnp.float32) * capacity + rank_row
    lane_id = lax.broadcasted_iota(jnp.int32, (blocks, slot_count), 1).astype(jnp.float32)
    pick_ref[...] = jnp.where(slot == lane_id, 1.0, 0.0).astype(jnp.bfloat16)
    line_id = lax.broadcasted_iota(jnp.int32, (slot_count, blocks), 0).astype(jnp.float32)
    placed = jnp.where(slot_row == line_id, 1.0, 0.0)
    place_ref[...] = placed.astype(jnp.bfloat16)
    tag = jnp.sum(placed * (target_ref[...].astype(jnp.float32) + 1.0), axis=1, keepdims=True)
    tag = jnp.broadcast_to(tag - 1.0, (slot_count, tags_ref.shape[2]))
    for p in range(tags_ref.shape[0]):
        tags_ref[p] = tag[p * capacity : (p + 1) * capacity, :]


def thirds(value):
    high = value.astype(jnp.bfloat16)
    rest = value - high.astype(jnp.float32)
    middle = rest.astype(jnp.bfloat16)
    low = (rest - middle.astype(jnp.float32)).astype(jnp.bfloat16)
    return high, middle, low


def select_rows(chooser, value):
    parts = [
        jnp.dot(chooser, part, preferred_element_type=jnp.float32) for part in thirds(value)
    ]
    return (parts[2] + parts[1]) + parts[0]


def couple_kernel(
    peers,
    width,
    wall_ref,
    prim_ref,
    normals_ref,
    index_ref,
    rbf_ref,
    pick_ref,
    place_ref,
    tags_ref,
    stiff_ref,
    coup_ref,
    inv_ref,
    disp_ref,
    res_ref,
    dif_ref,
    dens_ref,
    vel_ref,
    press_ref,
    fluid_ref,
    next_ref,
    motion_ref,
    low_ref,
    high_ref,
    side_ref,
    prior_ref,
    tag_in,
    load_out,
    load_in,
    reply_out,
    reply_in,
    stat_out,
    stat_in,
    loads,
    slots,
    solid,
    products,
    near_send,
    near_recv,
    tag_send,
    tag_recv,
    load_send,
    load_recv,
    stat_send,
    stat_recv,
    reply_send,
    reply_recv,
):
    me = lax.axis_index("group") * width + lax.axis_index("dev")
    blocks = index_ref.shape[0]
    count = disp_ref.shape[1]
    columns = res_ref.shape[0]
    capacity = tags_ref.shape[1]
    nodes = index_ref.shape[1]

    def place(peer):
        return (peer // width, peer % width)

    def hop(distance):
        return (me + distance) % peers

    barrier = pltpu.get_barrier_semaphore()

    def greet(step, carry):
        pl.semaphore_signal(barrier, inc=1, device_id=place(hop(step)), device_id_type=MESH)
        return carry

    lax.fori_loop(1, peers, greet, 0)
    products[...] = jnp.zeros_like(products)
    for m in range(columns):
        for n in range(m, columns):
            line = jnp.sum(jnp.sum(res_ref[m] * res_ref[n], axis=0), axis=0, keepdims=True)
            products[m * columns + n : m * columns + n + 1, :] = line
            products[n * columns + m : n * columns + m + 1, :] = line
    pl.semaphore_wait(barrier, peers - 1)

    def near(slot, src, dst, distance):
        return pltpu.make_async_remote_copy(
            src_ref=src,
            dst_ref=dst,
            send_sem=near_send.at[slot],
            recv_sem=near_recv.at[slot],
            device_id=place(hop(distance)),
            device_id_type=MESH,
        )

    wall_up = near(0, wall_ref.at[0], side_ref.at[0], 1)
    wall_down = near(1, wall_ref.at[0], side_ref.at[1], peers - 1)
    tail = prior_ref.shape[1]
    prior = near(2, disp_ref.at[:, pl.ds(count - tail, tail), :], prior_ref, 1)
    early, late = pl.ds(0, 3), pl.ds(3, 2)
    bulk_early = (
        near(3, prim_ref.at[early], low_ref.at[early], 1),
        near(4, prim_ref.at[early], high_ref.at[early], peers - 1),
    )
    bulk_late = (
        near(5, prim_ref.at[late], low_ref.at[late], 1),
        near(6, prim_ref.at[late], high_ref.at[late], peers - 1),
    )

    def spread(src, dst, send, recv, indexed):
        def begin(step, carry):
            peer = hop(step)
            pltpu.make_async_remote_copy(
                src_ref=src.at[peer] if indexed else src,
                dst_ref=dst.at[me],
                send_sem=send.at[step],
                recv_sem=recv.at[step],
                device_id=place(peer),
                device_id_type=MESH,
            ).start()
            return carry

        lax.fori_loop(1, peers, begin, 0)

    def gather(src, dst, send, recv, indexed):
        def finish(step, carry):
            pltpu.make_async_remote_copy(
                src_ref=src.at[hop(step)] if indexed else src,
                dst_ref=dst.at[hop(peers - step)],
                send_sem=send.at[step],
                recv_sem=recv.at[step],
                device_id=place(hop(step)),
                device_id_type=MESH,
            ).wait()
            return carry

        lax.fori_loop(1, peers, finish, 0)

    wall_up.start()
    wall_down.start()
    prior.start()
    spread(tags_ref, tag_in, tag_send, tag_recv, True)
    for copy in bulk_early:
        copy.start()
    tag_in[me] = tags_ref[me]

    wall_up.wait()
    wall_down.wait()

    def variant(i):
        return [wall_ref[i, k : k + 1, :] for k in range(5)]

    mid = variant(0)
    mirror = list(mid)
    mirror[3] = -mirror[3]
    beside = [[side_ref[j, k : k + 1, :] for k in range(5)] for j in range(2)]
    bottom = advance(mid, beside, (variant(3), variant(2)), (mirror, variant(1)))
    kinetic = bottom[1] * bottom[1] + bottom[2] * bottom[2] + bottom[3] * bottom[3]
    wall = (ratio_heat - 1.0) * (bottom[4] - 0.5 * kinetic / bottom[0])

    index = index_ref[...]
    low = index % nodes
    found = jnp.zeros(index.shape, jnp.float32)
    for part in range(wall.shape[1] // nodes):
        source = jnp.broadcast_to(wall[:, part * nodes : (part + 1) * nodes], index.shape)
        taken = jnp.take_along_axis(source, low, axis=1)
        found = jnp.where(index // nodes == part, taken, found)
    for c in range(3):
        loads[:, c, :] = found * normals_ref[c]
    for b in range(blocks):
        weighted = loads[b, 0:3, :].astype(jnp.bfloat16)
        loads[b, 0:3, :] = jnp.dot(weighted, rbf_ref[b], preferred_element_type=jnp.float32)
    spans = [slice(c * nodes, (c + 1) * nodes) for c in range(3)]
    for c in range(3):
        slots[:, spans[c]] = select_rows(place_ref[...], loads[:, c, :])
    for p in range(peers):
        load_out[p] = slots[p * capacity : (p + 1) * capacity, :]
    spread(load_out, load_in, load_send, load_recv, True)
    load_in[me] = load_out[me]

    prior.wait()
    first = (me > 0).astype(jnp.float32)
    for c in range(3):
        solid[:, c, :] = disp_ref[c]
    for t in range(count - 1, -1, -1):
        half = solid[t, 0:3, :].astype(jnp.bfloat16)
        earlier = solid[t - 1, 0:3, :] if t else prior_ref[:, tail - 1, :] * first
        part = lax.dot_general(half, stiff_ref[t], LAST, preferred_element_type=jnp.float32)
        part = part + lax.dot_general(
            earlier.astype(jnp.bfloat16), coup_ref[t], LAST, preferred_element_type=jnp.float32
        )
        solid[t, 0:3, :] = part

    gather(tags_ref, tag_in, tag_send, tag_recv, True)
    for p in range(peers):
        slots[p * capacity : (p + 1) * capacity, spans[0]] = tag_in[p]
    tags = slots[:, spans[0]]
    lane = lax.broadcasted_iota(jnp.int32, tags.shape, 1).astype(jnp.float32)
    chooser = (tags == lane).astype(jnp.float32)[:, 0:count].astype(jnp.bfloat16)
    turned = tags.T[0:count, :]
    line_id = lax.broadcasted_iota(jnp.int32, turned.shape, 0).astype(jnp.float32)
    collector = (turned == line_id).astype(jnp.float32).astype(jnp.bfloat16)

    gather(load_out, load_in, load_send, load_recv, True)
    for p in range(peers):
        slots[p * capacity : (p + 1) * capacity, :] = load_in[p]
    change = [
        -inv_ref[c] * (solid[:, c, :] - select_rows(collector, slots[:, spans[c]]))
        for c in range(3)
    ]
    for m in range(columns):
        line = sum(res_ref[m, c] * change[c] for c in range(3))
        at = columns * columns + m
        products[at : at + 1, :] = jnp.sum(line, axis=0, keepdims=True)
    stat_out[...] = jnp.sum(products[...].T, axis=0, keepdims=True)
    spread(stat_out, stat_in, stat_send, stat_recv, False)
    for copy in bulk_late:
        copy.start()
    stat_in[me] = stat_out[...]
    for c in range(3):
        next_ref[c] = disp_ref[c] + change[c]
    gather(stat_out, stat_in, stat_send, stat_recv, False)
    total = jnp.sum(stat_in[...], axis=0)
    shape = (columns, nodes)
    m_id = lax.broadcasted_iota(jnp.int32, shape, 0)
    n_id = lax.broadcasted_iota(jnp.int32, shape, 1)
    source = jnp.where(
        n_id < columns, m_id * columns + n_id, columns * columns + m_id
    )
    matrix = jnp.take_along_axis(jnp.broadcast_to(total, shape), source, axis=1)
    for k in range(columns):
        line = matrix[k : k + 1, :]
        scaled = line / matrix[k : k + 1, k : k + 1]
        matrix = jnp.where(m_id == k, scaled, matrix - matrix[:, k : k + 1] * scaled)
    mixing = -matrix[:, columns : columns + 1]
    for c in range(3):
        result = next_ref[c]
        for m in range(columns):
            result = result + dif_ref[m, c] * mixing[m : m + 1, :]
        next_ref[c] = result
        slots[:, spans[c]] = jnp.dot(
            chooser, result.astype(jnp.bfloat16), preferred_element_type=jnp.float32
        )
    for p in range(peers):
        reply_out[p] = slots[p * capacity : (p + 1) * capacity, :].astype(jnp.bfloat16)
    spread(reply_out, reply_in, reply_send, reply_recv, True)
    reply_in[me] = reply_out[me]
    for copy in bulk_early + bulk_late:
        copy.wait()
    flow_kernel(dens_ref, vel_ref, press_ref, low_ref, high_ref, fluid_ref)
    gather(reply_out, reply_in, reply_send, reply_recv, True)
    for p in range(peers):
        slots[p * capacity : (p + 1) * capacity, :] = reply_in[p].astype(jnp.float32)
    for c in range(3):
        rows = slots[:, spans[c]].astype(jnp.bfloat16)
        loads[:, c, :] = jnp.dot(pick_ref[...], rows, preferred_element_type=jnp.float32)
    for b in range(blocks):
        reply = loads[b, 0:3, :].astype(jnp.bfloat16)
        loads[b, 0:3, :] = lax.dot_general(
            reply, rbf_ref[b], LAST, preferred_element_type=jnp.float32
        )
    for c in range(3):
        motion_ref[c] = loads[:, c, :]


def rows_last(value):
    return jnp.swapaxes(value, -3, -2)


def on_device(
    density,
    velocity,
    pressure,
    rbf_blocks,
    correlation,
    normals,
    routes,
    targets,
    stiffness,
    coupling,
    inverse_diag,
    displacement,
    diff_res,
    diff_disp,
):
    f32, bf16 = jnp.float32, jnp.bfloat16
    width = lax.axis_size("dev")
    peers = lax.axis_size(AXES)
    blocks, nodes = correlation.shape
    count = displacement.shape[0]
    columns = diff_res.shape[0]
    height, depth = density.shape[1:]
    capacity = max(2, 2 * blocks // peers)
    slot_count = peers * capacity

    padded = -(-height // depth) * depth
    halo = jax.ShapeDtypeStruct((5, height, depth), bf16)
    vmem = pl.BlockSpec(memory_space=pltpu.VMEM)
    anywhere = pl.BlockSpec(memory_space=pl.ANY)
    dma = pltpu.SemaphoreType.DMA
    ends, prim, pick, put, tags = pl.pallas_call(
        functools.partial(prepare_kernel, capacity),
        out_shape=(
            jax.ShapeDtypeStruct((4, 8, padded), f32),
            halo,
            jax.ShapeDtypeStruct((blocks, slot_count), bf16),
            jax.ShapeDtypeStruct((slot_count, blocks), bf16),
            jax.ShapeDtypeStruct((peers, capacity, nodes), f32),
        ),
        in_specs=[vmem] * 6,
        out_specs=(vmem,) * 5,
        scratch_shapes=[pltpu.VMEM((padded, depth), f32)],
    )(density, velocity, pressure, routes, routes.reshape(1, blocks), targets.reshape(1, blocks))
    width_row = 3 * nodes
    fluid_next, disp_next, wall_motion = pl.pallas_call(
        functools.partial(couple_kernel, peers, width),
        out_shape=(
            jax.ShapeDtypeStruct((5,) + density.shape, f32),
            jax.ShapeDtypeStruct((3, count, nodes), f32),
            jax.ShapeDtypeStruct((3, blocks, nodes), f32),
        ),
        in_specs=[vmem, anywhere] + [vmem] * 15,
        out_specs=(vmem, vmem, vmem),
        scratch_shapes=[
            pltpu.VMEM(halo.shape, bf16),
            pltpu.VMEM(halo.shape, bf16),
            pltpu.VMEM((2, 8, padded), f32),
            pltpu.VMEM((3, 8, nodes), f32),
            pltpu.VMEM((peers, capacity, nodes), f32),
            pltpu.VMEM((peers, capacity, width_row), f32),
            pltpu.VMEM((peers, capacity, width_row), f32),
            pltpu.VMEM((peers, capacity, width_row), bf16),
            pltpu.VMEM((peers, capacity, width_row), bf16),
            pltpu.VMEM((1, nodes), f32),
            pltpu.VMEM((peers, 1, nodes), f32),
            pltpu.VMEM((blocks, 8, nodes), f32),
            pltpu.VMEM((slot_count, width_row), f32),
            pltpu.VMEM((count, 8, nodes), f32),
            pltpu.VMEM((nodes, nodes), f32),
            dma((7,)),
            dma((7,)),
        ]
        + [dma((peers,))] * 8,
        compiler_params=pltpu.CompilerParams(collective_id=0, has_side_effects=True),
    )(
        ends,
        prim,
        rows_last(normals),
        correlation,
        rbf_blocks,
        pick,
        put,
        tags,
        stiffness,
        coupling,
        rows_last(inverse_diag),
        rows_last(displacement),
        rows_last(diff_res),
        rows_last(diff_disp),
        density,
        velocity,
        pressure,
    )
    return (fluid_next, rows_last(disp_next), rows_last(wall_motion))


def solution(mesh):
    placed = (
        P(("group", "dev"), None, None),
        P(None, ("group", "dev"), None, None),
        P(("group", "dev"), None, None),
        P(("group", "dev"), None, None),
        P(("group", "dev"), None),
        P(("group", "dev"), None, None),
        P(("group", "dev"), None),
        P(("group", "dev")),
        P(("group", "dev"), None, None),
        P(("group", "dev"), None, None),
        P(("group", "dev"), None, None),
        P(("group", "dev"), None, None),
        P(None, ("group", "dev"), None, None),
        P(None, ("group", "dev"), None, None),
    )
    return jax.shard_map(
        on_device,
        mesh=mesh,
        in_specs=placed,
        out_specs=(
            P(None, ("group", "dev"), None, None),
            P(("group", "dev"), None, None),
            P(("group", "dev"), None, None),
        ),
        check_vma=False,
    )
```
